32 devices in a mesh: seq: 8 (over z, x), head: 4 (over y, core).
Axes of the slice: x: 2, y: 2, z: 4, core: 2. Of those that a mesh axis runs over, the one named last changes fastest.
Arguments:
- hidden_in: bfloat16 [256, 4096], P(None, 'seq'), may hold values from -6 to 6
- norm_gain: bfloat16 [1, 4096], P(None, 'seq'), may hold values from 0.25 to 1.75
- w_query: bfloat16 [4096, 4096], P('seq', 'head'), may hold values from -1 to 1
- w_key: bfloat16 [4096, 1024], P('seq', 'head'), may hold values from -1 to 1
- w_value: bfloat16 [4096, 1024], P('seq', 'head'), may hold values from -0.09375 to 0.09375
- w_out: bfloat16 [4096, 4096], P('head', 'seq'), may hold values from -0.09375 to 0.09375
- cache_keys: bfloat16 [32768, 8, 128], P('seq', 'head'), may hold values from -400 to 400
- cache_values: bfloat16 [32768, 8, 128], P('seq', 'head'), may hold values from -12 to 12
- lengths: int32 [8], replicated, may hold values from 512 to 4096, as said below
- span_start: int32 [1], replicated, may hold values from 0 to 256
Outputs:
- attn_out: bfloat16 [256, 4096], P('head', 'seq')
The draws below stay inside these ranges and needn't reach their ends.
Inputs may be any that keep to these rules, and one draw needn't show every extreme that they name: Slots 0 to lengths[s] - 1 of shard s are live, the others empty; in every draw some shard is full.
All inputs are finite; a program needn't handle non-finite values.
Results may differ from the reference program's by a relative error of at most 0.039.
The reference program's roundings to bfloat16 on the way count: a program that leaves them out, or rounds other values in their place, can miss the bound.
Values may be sent and summed in bfloat16 or wider, within the bound.
No kernel may reach another device: no remote copies, remote signals or barrier semaphores. Data moves between devices by JAX's collectives and lax.ppermute only.
A program may use at most 64 MiB of HBM per device.

```python
import math
import jax
import jax.numpy as jnp
from jax import lax

D = 4096
HEADS = 32
KV_HEADS = 8
HEAD_DIM = 128
SPAN = 256
CACHE_DEV = 4096
CACHE = 32768


def draw_lengths(key, part):
    key = jax.random.fold_in(key, 7)
    shard_count = CACHE // CACHE_DEV
    key_light, key_heavy, key_order = jax.random.split(key, 3)
    light_len = jax.random.randint(key_light, (shard_count,), CACHE_DEV // 8, CACHE_DEV // 3 + 1)
    heavy_len = jax.random.randint(key_heavy, (shard_count,), CACHE_DEV * 3 // 4, CACHE_DEV + 1)
    position_rank = jnp.argsort(jax.random.permutation(key_order, shard_count))
    lengths = jnp.where(position_rank < shard_count // 4, heavy_len, light_len)
    return jnp.where(position_rank == 0, CACHE_DEV, lengths).astype(jnp.int32)


def shared_projections(key):
    key_common, key_private = jax.random.split(jax.random.fold_in(key, 17), 2)
    group_size = HEADS // KV_HEADS
    spread = D ** (-0.5)
    common = jnp.clip(jax.random.normal(key_common, (D, KV_HEADS, 1, HEAD_DIM), jnp.float32), -6.0, 6.0) * spread
    private = jnp.clip(jax.random.normal(key_private, (D, KV_HEADS, group_size, HEAD_DIM), jnp.float32), -6.0, 6.0) * spread
    coupling = min(0.95, (math.log(0.4 * CACHE) + 0.8) / (2.005 * math.sqrt(HEAD_DIM)))
    query_part = coupling * common + math.sqrt(1.0 - coupling * coupling) * private
    return (query_part.reshape(D, HEADS * HEAD_DIM), common.reshape(D, KV_HEADS * HEAD_DIM))


def draw_w_query(key, part):
    return shared_projections(key)[0].astype(jnp.bfloat16)


def draw_w_key(key, part):
    return shared_projections(key)[1].astype(jnp.bfloat16)


def draw_cache_keys(key, part):
    key_base = jax.random.fold_in(jax.random.fold_in(key, 11), 0)
    normal_part = jnp.clip(jax.random.normal(key_base, (CACHE, KV_HEADS, HEAD_DIM), jnp.float32), -6.0, 6.0)
    return normal_part.astype(jnp.bfloat16)


def draw_cache_values(key, part):
    shard_count = CACHE // CACHE_DEV
    key_noise, key_shift = jax.random.split(jax.random.fold_in(key, 13), 2)
    shifts = jnp.clip(jax.random.normal(key_shift, (shard_count, 1, KV_HEADS, HEAD_DIM), jnp.float32), -4.0, 4.0)
    noise = jnp.clip(jax.random.normal(key_noise, (shard_count, CACHE_DEV, KV_HEADS, HEAD_DIM), jnp.float32), -4.0, 4.0)
    return (noise + shifts).reshape(CACHE, KV_HEADS, HEAD_DIM).astype(jnp.bfloat16)


def level_of(own_key, extent, shards, least, top_value):
    def one(axis_at, parts):
        draws = jax.random.uniform(jax.random.fold_in(jax.random.fold_in(own_key, 6), axis_at), (parts,), jnp.float32, least / len(shards), top_value / len(shards))
        return jnp.repeat(jnp.exp(draws), extent[axis_at] // parts).reshape((-1,) + (1,) * (len(extent) - axis_at - 1))

    factor_of = one(*shards[0])
    for cut in shards[1:]:
        factor_of = factor_of * one(*cut)
    return factor_of


def normal_values(stream_key, dims, scale, most, shards=(), kind=jnp.bfloat16):
    result = jax.random.normal(stream_key, dims, jnp.float32) * scale
    if len(shards) > 0:
        result = level_of(stream_key, dims, shards, -0.22, 0.18) * result
    return jnp.clip(result, min=-most, max=most).astype(kind)


def setup_inputs(seed: int = 0) -> dict:
    keys = jax.random.split(jax.random.key(seed), 11)
    hidden_in = normal_values(keys[0], (SPAN, D), 1.0, 6.0, ((1, 8),))
    norm_gain = jnp.clip(1.0 + 0.15 * jax.random.normal(keys[1], (1, D), jnp.float32), 0.25, 1.75).astype(jnp.bfloat16)
    w_query = draw_w_query(jax.random.fold_in(keys[10], 71), 0)
    w_key = draw_w_key(jax.random.fold_in(keys[10], 71), 0)
    w_value = normal_values(keys[4], (D, KV_HEADS * HEAD_DIM), D ** -0.5, 0.09375, ((0, 8), (1, 4)))
    w_out = normal_values(keys[5], (HEADS * HEAD_DIM, D), (HEADS * HEAD_DIM) ** -0.5, 0.09375, ((0, 4), (1, 8)))
    cache_keys = draw_cache_keys(jax.random.fold_in(keys[10], 71), 0)
    cache_values = draw_cache_values(jax.random.fold_in(keys[10], 71), 0)
    lengths = draw_lengths(jax.random.fold_in(keys[10], 71), 0)
    span_start = jax.random.randint(keys[9], (1,), 0, SPAN + 1).astype(jnp.int32)
    return dict(hidden_in=hidden_in, norm_gain=norm_gain, w_query=w_query, w_key=w_key, w_value=w_value, w_out=w_out, cache_keys=cache_keys, cache_values=cache_values, lengths=lengths, span_start=span_start)


rope_base = 500000.0
stretch = 64.0
initial_context = 8192.0
ramp_low = 1.0
ramp_high = 32.0
epsilon = 1e-05
negative = -1e+30

def rope_parts(positions, head_dim):
    half_dim = head_dim // 2
    indices = jnp.arange(half_dim, dtype=jnp.float32)
    base_freq = jnp.power(jnp.float32(rope_base), -2.0 * indices / head_dim)
    wavelength = 2.0 * math.pi / base_freq
    turn_count = initial_context / wavelength
    ramp_share = jnp.clip((turn_count - ramp_low) / (ramp_high - ramp_low), 0.0, 1.0)
    frequency = (1.0 - ramp_share) * base_freq / stretch + ramp_share * base_freq
    angles = positions[:, None] * frequency[None, :]
    mscale = 0.1 * math.log(stretch) + 1.0
    return (jnp.cos(angles) * mscale, jnp.sin(angles) * mscale)

def rotate(vectors, cosine, sine_part):
    half_dim = vectors.shape[-1] // 2
    lower_half = vectors[..., :half_dim]
    upper_half = vectors[..., half_dim:]
    cosine = cosine[:, None, :]
    sine_part = sine_part[:, None, :]
    return jnp.concatenate([lower_half * cosine - upper_half * sine_part, upper_half * cosine + lower_half * sine_part], -1)

def round_trip(values):
    return lax.optimization_barrier(values.astype(jnp.bfloat16)).astype(jnp.float32)

def attend(running, queries, key_block, value_block, visible):
    maxima, totals, weighted = running
    scores = jnp.einsum('tgrd,kgd->grtk', queries, key_block)
    scores = jnp.where(visible, scores, negative)
    new_max = jnp.maximum(maxima, lax.optimization_barrier(jnp.max(scores, axis=-1)))
    probability = jnp.where(visible, jnp.exp(scores - new_max[..., None]), 0.0)
    rescale = jnp.exp(maxima - new_max)
    totals = totals * rescale + lax.optimization_barrier(jnp.sum(probability, axis=-1))
    weighted = weighted * rescale[..., None] + jnp.einsum('grtk,kgd->grtd', round_trip(probability), value_block)
    return (new_max, totals, weighted)

def reference(hidden_in, norm_gain, w_query, w_key, w_value, w_out, cache_keys, cache_values, lengths, span_start):
    group_size = HEADS // KV_HEADS
    input_f32 = hidden_in.astype(jnp.float32)
    inv_rms = lax.rsqrt(lax.optimization_barrier(jnp.mean(input_f32 * input_f32, axis=1, keepdims=True)) + epsilon)
    normed = (input_f32 * inv_rms * norm_gain.astype(jnp.float32)).astype(jnp.bfloat16)
    queries = jnp.dot(normed, w_query, preferred_element_type=jnp.float32)
    new_keys = round_trip(jnp.dot(normed, w_key, preferred_element_type=jnp.float32))
    new_values = round_trip(jnp.dot(normed, w_value, preferred_element_type=jnp.float32))
    new_values = new_values.reshape(SPAN, KV_HEADS, HEAD_DIM)
    first_pos = jnp.sum(lengths).astype(jnp.int32) + span_start[0]
    query_pos = (first_pos + jnp.arange(SPAN, dtype=jnp.int32)).astype(jnp.float32)
    cosine, sine_part = rope_parts(query_pos, HEAD_DIM)
    rotated = rotate(queries.reshape(SPAN, HEADS, HEAD_DIM), cosine, sine_part) * HEAD_DIM ** (-0.5)
    query_f32 = round_trip(rotated).reshape(SPAN, KV_HEADS, group_size, HEAD_DIM)
    key_rot = round_trip(rotate(new_keys.reshape(SPAN, KV_HEADS, HEAD_DIM), cosine, sine_part))
    offsets = jnp.cumsum(lengths) - lengths
    block_len = math.gcd(CACHE, 4096)

    def sweep_block(running, block_index):
        block_start = block_index * block_len
        key_block = lax.dynamic_slice_in_dim(cache_keys, block_start, block_len, 0).astype(jnp.float32)
        value_block = lax.dynamic_slice_in_dim(cache_values, block_start, block_len, 0).astype(jnp.float32)
        slot_ids = block_start + jnp.arange(block_len, dtype=jnp.int32)
        shard_ids = slot_ids // CACHE_DEV
        slot_in_shard = slot_ids - shard_ids * CACHE_DEV
        occupied = slot_in_shard < jnp.take(lengths, shard_ids)
        positions = (jnp.take(offsets, shard_ids) + slot_in_shard).astype(jnp.float32)
        block_cos, block_sin = rope_parts(positions, HEAD_DIM)
        block_keys = round_trip(rotate(key_block, block_cos, block_sin))
        return (attend(running, query_f32, block_keys, value_block, occupied[None, None, None, :]), None)
    running = (jnp.full((KV_HEADS, group_size, SPAN), negative, jnp.float32), jnp.zeros((KV_HEADS, group_size, SPAN), jnp.float32), jnp.zeros((KV_HEADS, group_size, SPAN, HEAD_DIM), jnp.float32))
    running, leftover = lax.scan(sweep_block, running, jnp.arange(CACHE // block_len, dtype=jnp.int32))
    causal = jnp.arange(SPAN)[None, :] <= jnp.arange(SPAN)[:, None]
    maxima, totals, weighted = attend(running, query_f32, key_rot, new_values, causal[None, None])
    attended = (weighted / totals[..., None]).transpose(2, 0, 1, 3).reshape(SPAN, HEADS * HEAD_DIM)
    attended = attended.astype(jnp.bfloat16)
    return jnp.dot(attended, w_out, preferred_element_type=jnp.float32).astype(jnp.bfloat16)
```

```python
import functools
import math

import jax
import jax.numpy as jnp
import numpy as np
from jax import lax
from jax.experimental import pallas as pl
from jax.experimental.pallas import tpu as pltpu
from jax.sharding import PartitionSpec as P


rope_base = 500000.0
stretch = 64.0
initial_context = 8192.0
ramp_low = 1.0
ramp_high = 32.0
epsilon = 1e-05
negative = -1e30
LOG2E = math.log2(math.e)

f32 = jnp.float32
bf16 = jnp.bfloat16


def frequencies(head_dim):
    half = head_dim // 2
    base = rope_base ** (-2.0 * np.arange(half, dtype=np.float64) / head_dim)
    turns = initial_context * base / (2.0 * np.pi)
    share = np.clip((turns - ramp_low) / (ramp_high - ramp_low), 0.0, 1.0)
    return (1.0 - share) * base / stretch + share * base


def magnitude():
    return 0.1 * math.log(stretch) + 1.0


def split3(v):
    hi = v.astype(bf16).astype(f32)
    mid = (v - hi).astype(bf16).astype(f32)
    return hi, mid, v - hi - mid


def pack_rows(v):
    hi, mid, lo = split3(v)
    rows = lax.broadcasted_iota(jnp.int32, (16, v.shape[1]), 0)
    out = jnp.where(rows == 0, hi, jnp.where(rows == 1, mid, jnp.where(rows == 2, lo, 0.0)))
    return out.astype(bf16)


def unpack_rows(tile):
    t = tile.astype(f32)
    return t[0:1] + t[1:2] + t[2:3]


def project_kernel(n, hd, s_ref, x_ref, g_ref, wq_ref, wk_ref, wv_ref, *refs):
    outs, kv = refs[:n], refs[n]
    me = s_ref[0]
    span = x_ref.shape[0]
    rows = span // n
    x = x_ref[...].astype(f32)
    xg = (x * g_ref[...].astype(f32)).astype(bf16)
    sq = x * x
    hi = sq.astype(bf16)
    lo = (sq - hi.astype(f32)).astype(bf16)
    ones = jnp.ones((16, x.shape[1]), bf16)
    dims = (((1,), (1,)), ((), ()))
    sums = lax.dot_general(ones, hi, dims, preferred_element_type=f32)
    sums = sums + lax.dot_general(ones, lo, dims, preferred_element_type=f32)
    tail = pack_rows(sums[0:1])
    kw = wk_ref.shape[1]
    kv[:, :kw] = jnp.dot(xg, wk_ref[...], preferred_element_type=f32)
    kv[:, kw:] = jnp.dot(xg, wv_ref[...], preferred_element_type=f32)
    for k in range(n):
        peer = jnp.bitwise_xor(me, k)
        col = pl.multiple_of(peer * hd, hd)
        part = jnp.dot(xg, wq_ref[:, pl.ds(col, hd)], preferred_element_type=f32)
        outs[k][:hd, :] = part.T.astype(bf16)
        row = pl.multiple_of(peer * rows, rows)
        outs[k][hd : hd + rows, :] = kv[pl.ds(row, rows), :kw].astype(bf16)
        outs[k][hd + rows : hd + 2 * rows, :] = kv[pl.ds(row, rows), kw:].astype(bf16)
        outs[k][hd + 2 * rows :, :] = tail


def rotate_kernel(n, hd, width, s_ref, qc_ref, qs_ref, kc_ref, ks_ref, *refs):
    blocks, (q_ref, k_ref, v_ref) = refs[:n], refs[n:]
    me = s_ref[0]
    half = hd // 2
    span = q_ref.shape[1]
    rows = k_ref.shape[0]
    q = blocks[0][:hd, :].astype(f32)
    kv = blocks[0][hd : hd + 2 * rows, :].astype(f32)
    total = unpack_rows(blocks[0][hd + 2 * rows :, :])
    for b in blocks[1:]:
        q = q + b[:hd, :].astype(f32)
        kv = kv + b[hd : hd + 2 * rows, :].astype(f32)
        total = total + unpack_rows(b[hd + 2 * rows :, :])
    inv = lax.rsqrt(total / width + epsilon)
    q = q * inv
    c, s = qc_ref[...], qs_ref[...]
    scale = hd ** (-0.5) * LOG2E
    lo, up = q[:half], q[half:]
    q_ref[:half, :] = ((lo * c - up * s) * scale).astype(bf16)
    q_ref[half:, :] = ((up * c + lo * s) * scale).astype(bf16)
    lanes = lax.broadcasted_iota(jnp.int32, (rows, span), 1)
    subs = lax.broadcasted_iota(jnp.int32, (rows, span), 0)
    pick = jnp.where(lanes == subs + me * rows, jnp.broadcast_to(inv, (rows, span)), 0.0)
    col = jnp.sum(pick, axis=1, keepdims=True)
    key = (kv[:rows] * col).astype(bf16).astype(f32)
    val = kv[rows:] * col
    kc, ks = kc_ref[...], ks_ref[...]
    for g in range(k_ref.shape[1] // hd):
        u = key[:, g * hd : (g + 1) * hd]
        k_ref[:, g * hd : (g + 1) * hd] = (u * kc + pltpu.roll(u, half, 1) * ks).astype(bf16)
    v_ref[...] = val.T.astype(bf16)


def prepare_kernel(kv_heads, hd, s_ref, ac_ref, as_ref, bc_ref, bs_ref, k_ref, v_ref, kr_ref, vt_ref):
    blk = k_ref.shape[0]
    at = pl.program_id(0)
    fine = bc_ref.shape[0]
    steps = blk // fine
    half = hd // 2

    @pl.when(at * blk < s_ref[1])
    def _():
        bc, bs = bc_ref[...], bs_ref[...]
        lanes = lax.broadcasted_iota(jnp.int32, (1, hd), 1)
        sign = jnp.where(lanes < half, -1.0, 1.0)
        for j in range(steps):
            row = at * steps + j
            ac, asn = ac_ref[pl.ds(row, 1), :], as_ref[pl.ds(row, 1), :]
            c = ac * bc - asn * bs
            s = (asn * bc + ac * bs) * sign
            part = pl.ds(j * fine, fine)
            for g in range(kv_heads):
                u = k_ref[part, g, :].astype(f32)
                kr_ref[g, part, :] = (u * c + pltpu.roll(u, half, 1) * s).astype(bf16)
        for g in range(kv_heads):
            vt_ref[g, :, :] = v_ref[:, g, :].astype(f32).T.astype(bf16)


def attend_kernel(heads, blk, s_ref, kr_ref, vt_ref, kn_ref, vn_ref, *refs):
    qs, outs = refs[:heads], refs[heads : 2 * heads]
    m_ref, l_ref, acc_ref = refs[2 * heads :]
    me, live, g = s_ref[0], s_ref[1], s_ref[2]
    hd, span = qs[0].shape
    rows = kn_ref.shape[0]
    m_ref[...] = jnp.full_like(m_ref, negative)
    l_ref[...] = jnp.zeros_like(l_ref)
    acc_ref[...] = jnp.zeros_like(acc_ref)

    def step(keys, values, mask):
        for i in range(heads):
            s = jnp.dot(keys, qs[i][...], preferred_element_type=f32)
            if mask is not None:
                s = jnp.where(mask, s, negative)
            old = m_ref[i]
            new = jnp.maximum(old, jnp.max(s, axis=0, keepdims=True))
            p = jnp.exp2(s - new)
            if mask is not None:
                p = jnp.where(mask, p, 0.0)
            scale = jnp.exp2(old - new)
            m_ref[i] = new
            l_ref[i] = l_ref[i] * scale + jnp.sum(p, axis=0, keepdims=True)
            acc_ref[i] = acc_ref[i] * scale + jnp.dot(
                values, p.astype(bf16), preferred_element_type=f32
            )

    whole = live // blk

    @pl.loop(0, whole)
    def _(j):
        at = pl.multiple_of(j * blk, blk)
        step(kr_ref[0, pl.ds(at, blk), :], vt_ref[0, :, pl.ds(at, blk)], None)

    @pl.when(whole * blk < live)
    def _():
        at = pl.multiple_of(whole * blk, blk)
        slot = at + lax.broadcasted_iota(jnp.int32, (blk, span), 0)
        keep = lax.broadcasted_iota(jnp.int32, (hd, blk), 1) + at < live
        values = jnp.where(keep, vt_ref[0, :, pl.ds(at, blk)], jnp.zeros((hd, blk), bf16))
        step(kr_ref[0, pl.ds(at, blk), :], values, slot < live)

    token = lax.broadcasted_iota(jnp.int32, (rows, span), 1)
    fresh = me * rows + lax.broadcasted_iota(jnp.int32, (rows, span), 0)
    lane = pl.multiple_of(g * hd, hd)
    step(kn_ref[:, pl.ds(lane, hd)], vn_ref[pl.ds(lane, hd), :], fresh <= token)
    for i in range(heads):
        outs[i][:hd, :] = (acc_ref[i] / l_ref[i]).astype(bf16)
        outs[i][hd:, :] = pack_rows(m_ref[i] + jnp.log2(l_ref[i]))


def merge_kernel(n, hd, *refs):
    blocks, out = refs[:n], refs[n]
    lse = [unpack_rows(b[hd:, :]) for b in blocks]
    top = functools.reduce(jnp.maximum, lse)
    weights = [jnp.exp2(v - top) for v in lse]
    total = functools.reduce(jnp.add, weights)
    acc = blocks[0][:hd, :].astype(f32) * (weights[0] / total)
    for b, w in zip(blocks[1:], weights[1:]):
        acc = acc + b[:hd, :].astype(f32) * (w / total)
    out[...] = acc.astype(bf16)


def output_kernel(n, parts, hd, s_ref, w_ref, *refs):
    blocks, outs, acc = refs[:n], refs[n : n + parts], refs[n + parts]
    me, mine = s_ref[0], s_ref[3]
    total = None
    for k in range(n):
        row = pl.multiple_of(jnp.bitwise_xor(me, k) * hd, hd)
        a = blocks[k][...].astype(f32).T.astype(bf16)
        term = jnp.dot(a, w_ref[pl.ds(row, hd), :], preferred_element_type=f32)
        total = term if total is None else total + term
    acc[...] = total
    rows = acc.shape[0] // parts
    for j in range(parts):
        at = pl.multiple_of(jnp.bitwise_xor(mine, j) * rows, rows)
        outs[j][...] = acc[pl.ds(at, rows), :].astype(bf16)


def xor_send(value, axis, size, k):
    return lax.ppermute(value, axis, [(i, i ^ k) for i in range(size)])


def fast_local(
    hidden_in, norm_gain, w_query, w_key, w_value, w_out, cache_keys, cache_values, lengths, span_start
):
    n = lax.axis_size("seq")
    parts = lax.axis_size("head")
    me = lax.axis_index("seq")
    mine = lax.axis_index("head")
    span, width_local = hidden_in.shape
    slots, kv_heads, hd = cache_keys.shape
    half = hd // 2
    rows = span // n
    kw = kv_heads * hd
    far = n // 2
    width = width_local * n
    vmem = pl.BlockSpec(memory_space=pltpu.VMEM)
    smem = pl.BlockSpec(memory_space=pltpu.SMEM)

    shard_ids = jnp.arange(n, dtype=jnp.int32)
    offset = jnp.sum(jnp.where(shard_ids < me, lengths, 0))
    live = jnp.sum(jnp.where(shard_ids == me, lengths, 0))
    first_pos = jnp.sum(lengths) + span_start[0]
    side = me // far
    scal_far = jnp.stack([me, live, 1 - side, mine]).astype(jnp.int32)
    scal_near = jnp.stack([me, live, side, mine]).astype(jnp.int32)

    freq = frequencies(hd)
    fine = 64
    coarse = slots // fine
    mag = magnitude()
    freq32 = jnp.asarray(freq, f32)
    coarse_pos = offset + fine * jnp.arange(coarse, dtype=jnp.int32)
    token_pos = first_pos + jnp.arange(span, dtype=jnp.int32)
    new_pos = first_pos + me * rows + jnp.arange(rows, dtype=jnp.int32)
    freq2 = jnp.concatenate([freq32, freq32])
    ang_a = coarse_pos.astype(f32)[:, None] * freq2[None, :]
    a_cos, a_sin = jnp.cos(ang_a) * mag, jnp.sin(ang_a) * mag
    fine_ang = np.arange(fine)[:, None] * np.concatenate([freq, freq])[None, :]
    b_cos, b_sin = jnp.asarray(np.cos(fine_ang), f32), jnp.asarray(np.sin(fine_ang), f32)
    ang_q = freq32[:, None] * token_pos.astype(f32)[None, :]
    q_cos, q_sin = jnp.cos(ang_q) * mag, jnp.sin(ang_q) * mag
    ang_n = new_pos.astype(f32)[:, None] * freq2[None, :]
    sign = jnp.where(jnp.arange(hd) < half, -1.0, 1.0).astype(f32)
    n_cos, n_sin = jnp.cos(ang_n) * mag, jnp.sin(ang_n) * mag * sign

    block_rows = hd + 2 * rows + 16
    sends = pl.pallas_call(
        functools.partial(project_kernel, n, hd),
        out_shape=[jax.ShapeDtypeStruct((block_rows, span), bf16)] * n,
        in_specs=[smem] + [vmem] * 5,
        out_specs=[vmem] * n,
        scratch_shapes=[pltpu.VMEM((span, 2 * kw), f32)],
        name="project",
    )(scal_far, hidden_in, norm_gain, w_query, w_key, w_value)
    order = [k for k in range(far, n)] + [k for k in range(1, far)]
    got = {0: sends[0]}
    for k in order:
        got[k] = xor_send(sends[k], "seq", n, k)

    blk = 512
    grid = slots // blk
    last = lambda i, s: jnp.minimum(i, (s[1] - 1) // blk)
    whole = lambda i, s: (0, 0)
    k_rot, v_t = pl.pallas_call(
        functools.partial(prepare_kernel, kv_heads, hd),
        grid_spec=pltpu.PrefetchScalarGridSpec(
            num_scalar_prefetch=1,
            grid=(grid,),
            in_specs=[
                pl.BlockSpec((coarse, hd), whole),
                pl.BlockSpec((coarse, hd), whole),
                pl.BlockSpec((fine, hd), whole),
                pl.BlockSpec((fine, hd), whole),
                pl.BlockSpec((blk, kv_heads, hd), lambda i, s: (last(i, s), 0, 0)),
                pl.BlockSpec((blk, kv_heads, hd), lambda i, s: (last(i, s), 0, 0)),
            ],
            out_specs=[
                pl.BlockSpec((kv_heads, blk, hd), lambda i, s: (0, i, 0)),
                pl.BlockSpec((kv_heads, hd, blk), lambda i, s: (0, 0, i)),
            ],
        ),
        out_shape=[
            jax.ShapeDtypeStruct((kv_heads, slots, hd), bf16),
            jax.ShapeDtypeStruct((kv_heads, hd, slots), bf16),
        ],
        cost_estimate=pl.CostEstimate(
            flops=8 * slots * kw, transcendentals=0, bytes_accessed=8 * slots * kw
        ),
        name="prepare",
    )(scal_far, a_cos, a_sin, b_cos, b_sin, cache_keys, cache_values)

    q_own, k_new, v_new = pl.pallas_call(
        functools.partial(rotate_kernel, n, hd, width),
        out_shape=[
            jax.ShapeDtypeStruct((hd, span), bf16),
            jax.ShapeDtypeStruct((rows, kw), bf16),
            jax.ShapeDtypeStruct((kw, rows), bf16),
        ],
        in_specs=[smem] + [vmem] * (4 + n),
        out_specs=[vmem] * 3,
        name="rotate",
    )(scal_far, q_cos, q_sin, n_cos, n_sin, *[got[k] for k in range(n)])

    queries = {0: q_own}
    for k in order:
        queries[k] = xor_send(q_own, "seq", n, k)

    tile_rows = hd + 16
    pick = lambda i, s: (s[2], 0, 0)
    same = lambda i, s: (0, 0)

    def attend(scal, ks):
        heads = len(ks)
        return pl.pallas_call(
            functools.partial(attend_kernel, heads, blk),
            grid_spec=pltpu.PrefetchScalarGridSpec(
                num_scalar_prefetch=1,
                grid=(1,),
                in_specs=[
                    pl.BlockSpec((1, slots, hd), pick),
                    pl.BlockSpec((1, hd, slots), pick),
                    pl.BlockSpec((rows, kw), same),
                    pl.BlockSpec((kw, rows), same),
                ]
                + [pl.BlockSpec((hd, span), same)] * heads,
                out_specs=[pl.BlockSpec((tile_rows, span), same)] * heads,
                scratch_shapes=[
                    pltpu.VMEM((heads, 1, span), f32),
                    pltpu.VMEM((heads, 1, span), f32),
                    pltpu.VMEM((heads, hd, span), f32),
                ],
            ),
            out_shape=[jax.ShapeDtypeStruct((tile_rows, span), bf16)] * heads,
            cost_estimate=pl.CostEstimate(
                flops=4 * heads * span * slots * hd,
                transcendentals=heads * span * slots,
                bytes_accessed=4 * slots * hd,
            ),
            name="attend",
        )(scal, k_rot, v_t, k_new, v_new, *[queries[k] for k in ks])

    far_ks = list(range(far, n))
    near_ks = list(range(far))
    partial = dict(zip(far_ks, attend(scal_far, far_ks)))
    merged_in = {k: xor_send(partial[k], "seq", n, k) for k in far_ks}
    partial.update(zip(near_ks, attend(scal_near, near_ks)))
    for k in near_ks[1:]:
        merged_in[k] = xor_send(partial[k], "seq", n, k)
    merged_in[0] = partial[0]
    attended = pl.pallas_call(
        functools.partial(merge_kernel, n, hd),
        out_shape=jax.ShapeDtypeStruct((hd, span), bf16),
        in_specs=[vmem] * n,
        out_specs=vmem,
        name="merge",
    )(*[merged_in[k] for k in range(n)])

    gathered = {0: attended}
    for k in order:
        gathered[k] = xor_send(attended, "seq", n, k)
    cols = w_out.shape[1]
    outs = pl.pallas_call(
        functools.partial(output_kernel, n, parts, hd),
        out_shape=[jax.ShapeDtypeStruct((span // parts, cols), bf16)] * parts,
        in_specs=[smem] + [vmem] * (1 + n),
        out_specs=[vmem] * parts,
        scratch_shapes=[pltpu.VMEM((span, cols), f32)],
        name="outproj",
    )(scal_far, w_out, *[gathered[k] for k in range(n)])
    total = outs[0].astype(f32)
    for j in range(1, parts):
        total = total + xor_send(outs[j], "head", parts, j).astype(f32)
    return total.astype(bf16)


def rope_parts(positions, head_dim):
    angles = positions[:, None] * jnp.asarray(frequencies(head_dim), f32)[None, :]
    return (jnp.cos(angles) * magnitude(), jnp.sin(angles) * magnitude())


def rotate(vectors, cosine, sine_part):
    half_dim = vectors.shape[-1] // 2
    lower_half = vectors[..., :half_dim]
    upper_half = vectors[..., half_dim:]
    cosine = cosine[:, None, :]
    sine_part = sine_part[:, None, :]
    return jnp.concatenate(
        [
            lower_half * cosine - upper_half * sine_part,
            upper_half * cosine + lower_half * sine_part,
        ],
        -1,
    )


def round_trip(values):
    return lax.optimization_barrier(values.astype(bf16)).astype(f32)


def attend_block(running, queries, key_block, value_block, visible):
    maxima, totals, weighted = running
    scores = jnp.einsum("tgrd,kgd->grtk", queries, key_block, preferred_element_type=f32)
    scores = jnp.where(visible, scores, negative)
    new_max = jnp.maximum(maxima, jnp.max(scores, axis=-1))
    probability = jnp.where(visible, jnp.exp(scores - new_max[..., None]), 0.0)
    rescale = jnp.exp(maxima - new_max)
    totals = totals * rescale + jnp.sum(probability, axis=-1)
    weighted = weighted * rescale[..., None] + jnp.einsum(
        "grtk,kgd->grtd", probability.astype(bf16), value_block, preferred_element_type=f32
    )
    return (new_max, totals, weighted)


def general_local(
    hidden_in, norm_gain, w_query, w_key, w_value, w_out, cache_keys, cache_values, lengths, span_start
):
    seq_count = lax.axis_size("seq")
    my_index = lax.axis_index("seq")
    span_len = hidden_in.shape[0]
    width = hidden_in.shape[1] * seq_count
    local_kv = cache_keys.shape[1]
    head_dim = cache_keys.shape[2]
    group_size = w_query.shape[1] // (local_kv * head_dim)
    kv_cols = w_key.shape[1]
    row_count = span_len // seq_count
    first_new = my_index * row_count
    input_f32 = hidden_in.astype(f32)
    square_sums = lax.psum(jnp.sum(input_f32 * input_f32, axis=1), "seq")
    inv_rms = lax.rsqrt(square_sums[:, None] / width + epsilon)
    normed = (input_f32 * inv_rms * norm_gain.astype(f32)).astype(bf16)
    queries = lax.psum(jnp.dot(normed, w_query, preferred_element_type=f32), "seq")
    kv_own = lax.psum_scatter(
        jnp.concatenate(
            [
                jnp.dot(normed, w_key, preferred_element_type=f32),
                jnp.dot(normed, w_value, preferred_element_type=f32),
            ],
            1,
        ),
        "seq",
        scatter_dimension=0,
        tiled=True,
    )
    key_own = kv_own[:, :kv_cols]
    value_own = kv_own[:, kv_cols:]
    shard_ids = jnp.arange(lengths.shape[0], dtype=jnp.int32)
    offset = jnp.sum(jnp.where(shard_ids < my_index, lengths, 0))
    live_count = jnp.sum(jnp.where(shard_ids == my_index, lengths, 0))
    first_pos = jnp.sum(lengths) + span_start[0]
    query_pos = (first_pos + jnp.arange(span_len, dtype=jnp.int32)).astype(f32)
    cosine, sine_part = rope_parts(query_pos, head_dim)
    rotated = rotate(
        queries.reshape(span_len, local_kv * group_size, head_dim), cosine, sine_part
    ) * head_dim ** (-0.5)
    query_low = rotated.astype(bf16).reshape(span_len, local_kv, group_size, head_dim)
    my_keys = round_trip(key_own).reshape(row_count, local_kv, head_dim)
    my_values = value_own.astype(bf16).reshape(row_count, local_kv, head_dim)
    new_pos = (first_pos + first_new + jnp.arange(row_count, dtype=jnp.int32)).astype(f32)
    new_cos, new_sin = rope_parts(new_pos, head_dim)
    new_key_rot = rotate(my_keys, new_cos, new_sin).astype(bf16)
    block_len = math.gcd(cache_keys.shape[0], 1024)

    def sweep_block(block_index, running):
        block_start = block_index * block_len
        key_block = lax.dynamic_slice_in_dim(cache_keys, block_start, block_len, 0).astype(f32)
        value_block = lax.dynamic_slice_in_dim(cache_values, block_start, block_len, 0)
        slot_ids = block_start + jnp.arange(block_len, dtype=jnp.int32)
        occupied = slot_ids < live_count
        positions = (offset + slot_ids).astype(f32)
        block_cos, block_sin = rope_parts(positions, head_dim)
        block_keys = rotate(key_block, block_cos, block_sin).astype(bf16)
        return attend_block(
            running, query_low, block_keys, value_block, occupied[None, None, None, :]
        )

    running = (
        jnp.full((local_kv, group_size, span_len), negative, f32),
        jnp.zeros((local_kv, group_size, span_len), f32),
        jnp.zeros((local_kv, group_size, span_len, head_dim), f32),
    )
    running = lax.fori_loop(0, cache_keys.shape[0] // block_len, sweep_block, running)
    query_rows = jnp.arange(span_len, dtype=jnp.int32)[:, None]
    key_rows = first_new + jnp.arange(row_count, dtype=jnp.int32)[None, :]
    maxima, totals, weighted = attend_block(
        running, query_low, new_key_rot, my_values, (key_rows <= query_rows)[None, None]
    )
    global_max = lax.pmax(maxima, "seq")
    rescale = jnp.exp(maxima - global_max)
    totals, weighted = lax.psum((totals * rescale, weighted * rescale[..., None]), "seq")
    attended = (
        (weighted / totals[..., None])
        .transpose(2, 0, 1, 3)
        .reshape(span_len, local_kv * group_size * head_dim)
    )
    partial_out = jnp.dot(attended.astype(bf16), w_out, preferred_element_type=f32)
    return lax.psum_scatter(partial_out.astype(bf16), "head", scatter_dimension=0, tiled=True)


def local(hidden_in, norm_gain, w_query, w_key, w_value, w_out, cache_keys, cache_values, lengths, span_start):
    args = (
        hidden_in, norm_gain, w_query, w_key, w_value, w_out, cache_keys, cache_values, lengths, span_start
    )
    n, parts = lax.axis_size("seq"), lax.axis_size("head")
    span = hidden_in.shape[0]
    slots, kv_heads, hd = cache_keys.shape
    fits = (
        n & (n - 1) == 0
        and parts & (parts - 1) == 0
        and kv_heads == 2
        and w_query.shape[1] == n * hd
        and kv_heads * hd == span
        and hd % 128 == 0
        and span % (32 * n) == 0
        and span % (16 * parts) == 0
        and slots % 512 == 0
    )
    return (fast_local if fits else general_local)(*args)


def solution(mesh):
    return jax.shard_map(
        local,
        mesh=mesh,
        in_specs=(
            P(None, "seq"),
            P(None, "seq"),
            P("seq", "head"),
            P("seq", "head"),
            P("seq", "head"),
            P("head", "seq"),
            P("seq", "head", None),
            P("seq", "head", None),
            P(),
            P(),
        ),
        out_specs=P("head", "seq"),
        check_vma=False,
    )
```

```python
import functools
import math

import jax
import jax.numpy as jnp
import numpy as np
from jax import lax
from jax.experimental import pallas as pl
from jax.experimental.pallas import tpu as pltpu
from jax.sharding import PartitionSpec as P


rope_base = 500000.0
stretch = 64.0
initial_context = 8192.0
ramp_low = 1.0
ramp_high = 32.0
epsilon = 1e-05
negative = -1e30
LOG2E = math.log2(math.e)

f32 = jnp.float32
bf16 = jnp.bfloat16


def frequencies(head_dim):
    half = head_dim // 2
    base = rope_base ** (-2.0 * np.arange(half, dtype=np.float64) / head_dim)
    turns = initial_context * base / (2.0 * np.pi)
    share = np.clip((turns - ramp_low) / (ramp_high - ramp_low), 0.0, 1.0)
    return (1.0 - share) * base / stretch + share * base


def magnitude():
    return 0.1 * math.log(stretch) + 1.0


def split3(v):
    hi = v.astype(bf16).astype(f32)
    mid = (v - hi).astype(bf16).astype(f32)
    return hi, mid, v - hi - mid


def pack_rows(v):
    hi, mid, lo = split3(v)
    rows = lax.broadcasted_iota(jnp.int32, (16, v.shape[1]), 0)
    out = jnp.where(rows == 0, hi, jnp.where(rows == 1, mid, jnp.where(rows == 2, lo, 0.0)))
    return out.astype(bf16)


def unpack_rows(tile):
    t = tile.astype(f32)
    return t[0:1] + t[1:2] + t[2:3]


def turn(a, b):
    return a[0] * b[0] - a[1] * b[1], a[1] * b[0] + a[0] * b[1]


def phase_row(position, bc_ref, bs_ref):
    bits = bc_ref.shape[0]
    place = lax.broadcasted_iota(jnp.int32, bc_ref.shape, 0)
    on = jnp.bitwise_and(jnp.right_shift(jnp.full(bc_ref.shape, position, jnp.int32), place), 1) == 1
    c = jnp.where(on, bc_ref[...], 1.0)
    s = jnp.where(on, bs_ref[...], 0.0)
    while bits > 1:
        bits //= 2
        c, s = turn((c[:bits], s[:bits]), (c[bits:], s[bits:]))
    return c, s


def length_sums(n, me, len_ref):
    offset, total = jnp.int32(0), jnp.int32(0)
    for r in range(n):
        offset = offset + jnp.where(r < me, len_ref[r], 0)
        total = total + len_ref[r]
    return offset, total


def project_kernel(n, hd, x_ref, g_ref, wq_ref, wk_ref, wv_ref, *refs):
    outs, kv = refs[:n], refs[n]
    me = lax.axis_index("seq")
    span = x_ref.shape[0]
    rows = span // n
    x = x_ref[...].astype(f32)
    xg = (x * g_ref[...].astype(f32)).astype(bf16)
    sq = x * x
    hi = sq.astype(bf16)
    lo = (sq - hi.astype(f32)).astype(bf16)
    ones = jnp.ones((16, x.shape[1]), bf16)
    dims = (((1,), (1,)), ((), ()))
    sums = lax.dot_general(ones, hi, dims, preferred_element_type=f32)
    sums = sums + lax.dot_general(ones, lo, dims, preferred_element_type=f32)
    tail = pack_rows(sums[0:1])
    kw = wk_ref.shape[1]
    kv[:, :kw] = jnp.dot(xg, wk_ref[...], preferred_element_type=f32)
    kv[:, kw:] = jnp.dot(xg, wv_ref[...], preferred_element_type=f32)
    for k in range(n):
        peer = jnp.bitwise_xor(me, k)
        col = pl.multiple_of(peer * hd, hd)
        part = jnp.dot(xg, wq_ref[:, pl.ds(col, hd)], preferred_element_type=f32)
        outs[k][:hd, :] = part.T.astype(bf16)
        row = pl.multiple_of(peer * rows, rows)
        outs[k][hd : hd + rows, :] = kv[pl.ds(row, rows), :kw].astype(bf16)
        outs[k][hd + rows : hd + 2 * rows, :] = kv[pl.ds(row, rows), kw:].astype(bf16)
        outs[k][hd + 2 * rows :, :] = tail


def rotate_kernel(
    n, hd, width, len_ref, start_ref, tc_ref, ts_ref, nc_ref, ns_ref, bc_ref, bs_ref, *refs
):
    blocks, (q_ref, k_ref, v_ref) = refs[:n], refs[n:]
    me = lax.axis_index("seq")
    half = hd // 2
    span = q_ref.shape[1]
    rows = k_ref.shape[0]
    _, total_len = length_sums(n, me, len_ref)
    pc, ps = phase_row(total_len + start_ref[0], bc_ref, bs_ref)
    pc, ps = pc * magnitude(), ps * magnitude()
    q = blocks[0][:hd, :].astype(f32)
    kv = blocks[0][hd : hd + 2 * rows, :].astype(f32)
    total = unpack_rows(blocks[0][hd + 2 * rows :, :])
    for b in blocks[1:]:
        q = q + b[:hd, :].astype(f32)
        kv = kv + b[hd : hd + 2 * rows, :].astype(f32)
        total = total + unpack_rows(b[hd + 2 * rows :, :])
    inv = lax.rsqrt(total / width + epsilon)
    diag = lax.broadcasted_iota(jnp.int32, (half, hd), 0) == lax.broadcasted_iota(
        jnp.int32, (half, hd), 1
    )
    column = lambda r: jnp.sum(
        jnp.where(diag, jnp.broadcast_to(r, (half, hd)), 0.0), axis=1, keepdims=True
    )
    c, s = turn((column(pc), column(ps)), (tc_ref[...], ts_ref[...]))
    gain = inv * (hd ** (-0.5) * LOG2E)
    lo, up = q[:half] * gain, q[half:] * gain
    q_ref[:half, :] = (lo * c - up * s).astype(bf16)
    q_ref[half:, :] = (up * c + lo * s).astype(bf16)
    lanes = lax.broadcasted_iota(jnp.int32, (rows, span), 1)
    subs = lax.broadcasted_iota(jnp.int32, (rows, span), 0)
    pick = jnp.where(lanes == subs + me * rows, jnp.broadcast_to(inv, (rows, span)), 0.0)
    col = jnp.sum(pick, axis=1, keepdims=True)
    key = (kv[:rows] * col).astype(bf16).astype(f32)
    val = kv[rows:] * col
    mine = pl.ds(pl.multiple_of(me * rows, rows), rows)
    kc, ks = turn((pc, ps), (nc_ref[mine, :], ns_ref[mine, :]))
    ks = jnp.where(lax.broadcasted_iota(jnp.int32, (rows, hd), 1) < half, -ks, ks)
    for g in range(k_ref.shape[1] // hd):
        u = key[:, g * hd : (g + 1) * hd]
        k_ref[:, g * hd : (g + 1) * hd] = (u * kc + pltpu.roll(u, half, 1) * ks).astype(bf16)
    v_ref[...] = val.T.astype(bf16)


def prepare_kernel(
    n, hd, len_ref, ac_ref, as_ref, fc_ref, fs_ref, bc_ref, bs_ref, k_ref, v_ref, kr_ref, vt_ref
):
    me = lax.axis_index("seq")
    at = pl.program_id(0)
    blk = kr_ref.shape[1]
    fine = fc_ref.shape[0]
    half = hd // 2
    pair = 2 * hd
    offset, _ = length_sums(n, me, len_ref)

    @pl.when(at * blk < len_ref[me])
    def _():
        pc, ps = phase_row(offset, bc_ref, bs_ref)
        pc, ps = pc * magnitude(), ps * magnitude()
        fc, fs = fc_ref[...], fs_ref[...]
        sign = jnp.where(lax.broadcasted_iota(jnp.int32, (1, hd), 1) < half, -1.0, 1.0)
        r = lax.broadcasted_iota(jnp.int32, (pair, pair), 0)
        c = lax.broadcasted_iota(jnp.int32, (pair, pair), 1)
        perm = jnp.where(c == 2 * (r % hd) + r // hd, 1.0, 0.0).astype(bf16)
        for j in range(blk // hd):
            cos, sin = [], []
            for t in range(hd // fine):
                row = pl.ds(at * (blk // fine) + j * (hd // fine) + t, 1)
                base = turn((pc, ps), (ac_ref[row, :], as_ref[row, :]))
                cc, ss = turn(base, (fc, fs))
                cos.append(cc)
                sin.append(ss * sign)
            cos, sin = jnp.concatenate(cos, 0), jnp.concatenate(sin, 0)
            part = slice(j * hd, (j + 1) * hd)
            u = jnp.dot(perm, k_ref[j * pair : (j + 1) * pair, :], preferred_element_type=f32)
            w = jnp.dot(perm, v_ref[j * pair : (j + 1) * pair, :], preferred_element_type=f32)
            w = w.astype(bf16)
            for g in range(2):
                x = u[g * hd : (g + 1) * hd]
                kr_ref[g, part, :] = (x * cos + pltpu.roll(x, half, 1) * sin).astype(bf16)
                vt_ref[g, :, part] = w[g * hd : (g + 1) * hd].T


def attend_kernel(far, flip, heads, blk, nch, len_ref, kr_hbm, vt_hbm, kn_ref, vn_ref, *refs):
    qs, outs = refs[:heads], refs[heads : 2 * heads]
    m_ref, l_ref, acc_ref, mx_ref, sa, sb, k_ref, v_ref, qx_ref, bias_ref, sem = refs[2 * heads :]
    me = lax.axis_index("seq")
    g = jnp.bitwise_xor(me // far, flip)
    live = len_ref[me]
    hd, span = qs[0].shape
    rows = kn_ref.shape[0]
    ch = blk // nch
    count = pl.cdiv(live, blk)
    copy_k = pltpu.make_async_copy(kr_hbm.at[g], k_ref, sem.at[0])
    copy_v = pltpu.make_async_copy(vt_hbm.at[g], v_ref, sem.at[1])
    copy_k.start()
    copy_v.start()
    m_ref[...] = jnp.full_like(m_ref, negative)
    l_ref[...] = jnp.zeros_like(l_ref)
    acc_ref[...] = jnp.zeros_like(acc_ref)
    unit = jnp.where(lax.broadcasted_iota(jnp.int32, (hd, span), 0) == 0, 1.0, 0.0).astype(bf16)
    for i in range(heads):
        qx_ref[i, :hd, :] = qs[i][...]
        qx_ref[i, hd:, :] = unit
    slot = lax.broadcasted_iota(jnp.int32, (blk, hd), 0) + (count - 1) * blk
    lane = lax.broadcasted_iota(jnp.int32, (blk, hd), 1)
    bias_ref[0] = jnp.zeros((blk, hd), bf16)
    bias_ref[1] = jnp.where((lane == 0) & (slot >= live), negative, 0.0).astype(bf16)
    copy_k.wait()
    copy_v.wait()
    bufs = (sa, sb)

    def score(i, buf, j, c):
        at = pl.multiple_of(j * blk + c * ch, ch)
        last = (j == count - 1).astype(jnp.int32)
        keys = jnp.concatenate([k_ref[pl.ds(at, ch), :], bias_ref[last, c * ch : (c + 1) * ch, :]], 1)
        s = jnp.dot(keys, qx_ref[i], preferred_element_type=f32)
        buf[c * ch : (c + 1) * ch, :] = s
        return jnp.max(s, axis=0, keepdims=True)

    def stage(i, j, i_next, j_next):
        cur, nxt = bufs[i % 2], bufs[(i + 1) % 2]
        old = m_ref[i]
        new = jnp.maximum(old, mx_ref[i % 2])
        scale = jnp.exp2(old - new)
        m_ref[i] = new
        tot, acc, top = l_ref[i] * scale, acc_ref[i] * scale, None
        for c in range(nch):
            t = score(i_next, nxt, j_next, c)
            top = t if top is None else jnp.maximum(top, t)
            p = jnp.exp2(cur[c * ch : (c + 1) * ch, :] - new)
            tot = tot + jnp.sum(p, axis=0, keepdims=True)
            at = pl.multiple_of(j * blk + c * ch, ch)
            acc = acc + jnp.dot(v_ref[:, pl.ds(at, ch)], p.astype(bf16), preferred_element_type=f32)
        l_ref[i], acc_ref[i], mx_ref[(i + 1) % 2] = tot, acc, top

    mx_ref[0] = functools.reduce(jnp.maximum, [score(0, sa, 0, c) for c in range(nch)])

    @pl.loop(0, count)
    def _(j):
        later = jnp.minimum(j + 1, count - 1)
        for i in range(heads):
            stage(i, j, (i + 1) % heads, j if i + 1 < heads else later)

    token = lax.broadcasted_iota(jnp.int32, (rows, span), 1)
    fresh = me * rows + lax.broadcasted_iota(jnp.int32, (rows, span), 0)
    mask = fresh <= token
    cols = pl.ds(pl.multiple_of(g * hd, hd), hd)
    keys, values = kn_ref[:, cols], vn_ref[cols, :]
    for i in range(heads):
        s = jnp.where(mask, jnp.dot(keys, qs[i][...], preferred_element_type=f32), negative)
        old = m_ref[i]
        new = jnp.maximum(old, jnp.max(s, axis=0, keepdims=True))
        p = jnp.where(mask, jnp.exp2(s - new), 0.0)
        scale = jnp.exp2(old - new)
        total = l_ref[i] * scale + jnp.sum(p, axis=0, keepdims=True)
        acc = acc_ref[i] * scale + jnp.dot(values, p.astype(bf16), preferred_element_type=f32)
        outs[i][:hd, :] = (acc / total).astype(bf16)
        outs[i][hd:, :] = pack_rows(new + jnp.log2(total))


def merge_kernel(n, hd, *refs):
    blocks, out = refs[:n], refs[n]
    lse = [unpack_rows(b[hd:, :]) for b in blocks]
    top = functools.reduce(jnp.maximum, lse)
    weights = [jnp.exp2(v - top) for v in lse]
    total = functools.reduce(jnp.add, weights)
    acc = blocks[0][:hd, :].astype(f32) * (weights[0] / total)
    for b, w in zip(blocks[1:], weights[1:]):
        acc = acc + b[:hd, :].astype(f32) * (w / total)
    out[...] = acc.astype(bf16)


def output_kernel(n, parts, hd, w_ref, *refs):
    blocks, outs, acc = refs[:n], refs[n : n + parts], refs[n + parts]
    me, mine = lax.axis_index("seq"), lax.axis_index("head")
    total = None
    for k in range(n):
        row = pl.multiple_of(jnp.bitwise_xor(me, k) * hd, hd)
        a = blocks[k][...].T
        term = jnp.dot(a, w_ref[pl.ds(row, hd), :], preferred_element_type=f32)
        total = term if total is None else total + term
    acc[...] = total
    rows = acc.shape[0] // parts
    for j in range(parts):
        at = pl.multiple_of(jnp.bitwise_xor(mine, j) * rows, rows)
        outs[j][...] = acc[pl.ds(at, rows), :].astype(bf16)


def xor_send(value, axis, size, k):
    return lax.ppermute(value, axis, [(i, i ^ k) for i in range(size)])


def circle(positions, freq):
    angles = np.asarray(positions, np.float64)[:, None] * np.concatenate([freq, freq])[None, :]
    return jnp.asarray(np.cos(angles), f32), jnp.asarray(np.sin(angles), f32)


def fast_local(
    hidden_in, norm_gain, w_query, w_key, w_value, w_out, cache_keys, cache_values, lengths, span_start
):
    n = lax.axis_size("seq")
    parts = lax.axis_size("head")
    span, width_local = hidden_in.shape
    slots, kv_heads, hd = cache_keys.shape
    half = hd // 2
    rows = span // n
    kw = kv_heads * hd
    far = n // 2
    width = width_local * n
    vmem = pl.BlockSpec(memory_space=pltpu.VMEM)
    smem = pl.BlockSpec(memory_space=pltpu.SMEM)

    freq = frequencies(hd)
    fine = 64
    b_cos, b_sin = circle(2.0 ** np.arange(32), freq)
    a_cos, a_sin = circle(fine * np.arange(slots // fine), freq)
    f_cos, f_sin = circle(np.arange(fine), freq)
    n_cos, n_sin = circle(np.arange(span), freq)
    t_cos, t_sin = n_cos[:, :half].T, n_sin[:, :half].T

    block_rows = hd + 2 * rows + 16
    sends = pl.pallas_call(
        functools.partial(project_kernel, n, hd),
        out_shape=[jax.ShapeDtypeStruct((block_rows, span), bf16)] * n,
        in_specs=[vmem] * 5,
        out_specs=[vmem] * n,
        scratch_shapes=[pltpu.VMEM((span, 2 * kw), f32)],
        name="project",
    )(hidden_in, norm_gain, w_query, w_key, w_value)
    order = [k for k in range(far, n)] + [k for k in range(1, far)]
    got = {0: sends[0]}
    for k in order:
        got[k] = xor_send(sends[k], "seq", n, k)

    step = 2048
    whole = lambda i: (0, 0)
    consts = (a_cos, a_sin, f_cos, f_sin, b_cos, b_sin)
    k_rot, v_t = pl.pallas_call(
        functools.partial(prepare_kernel, n, hd),
        grid=(slots // step,),
        in_specs=[smem]
        + [pl.BlockSpec(v.shape, whole) for v in consts]
        + [pl.BlockSpec((step * kv_heads, hd), lambda i: (i, 0))] * 2,
        out_specs=[
            pl.BlockSpec((kv_heads, step, hd), lambda i: (0, i, 0)),
            pl.BlockSpec((kv_heads, hd, step), lambda i: (0, 0, i)),
        ],
        out_shape=[
            jax.ShapeDtypeStruct((kv_heads, slots, hd), bf16),
            jax.ShapeDtypeStruct((kv_heads, hd, slots), bf16),
        ],
        cost_estimate=pl.CostEstimate(
            flops=8 * slots * kw, transcendentals=0, bytes_accessed=8 * slots * kw
        ),
        name="prepare",
    )(
        lengths,
        *consts,
        cache_keys.reshape(slots * kv_heads, hd),
        cache_values.reshape(slots * kv_heads, hd),
    )

    q_own, k_new, v_new = pl.pallas_call(
        functools.partial(rotate_kernel, n, hd, width),
        out_shape=[
            jax.ShapeDtypeStruct((hd, span), bf16),
            jax.ShapeDtypeStruct((rows, kw), bf16),
            jax.ShapeDtypeStruct((kw, rows), bf16),
        ],
        in_specs=[smem] * 2 + [vmem] * (6 + n),
        out_specs=[vmem] * 3,
        name="rotate",
    )(lengths, span_start, t_cos, t_sin, n_cos, n_sin, b_cos, b_sin, *[got[k] for k in range(n)])

    queries = {0: q_own}
    for k in order:
        queries[k] = xor_send(q_own, "seq", n, k)

    tile_rows = hd + 16
    blk, nch = 1024, 4

    def attend(flip, ks):
        heads = len(ks)
        return pl.pallas_call(
            functools.partial(attend_kernel, far, flip, heads, blk, nch),
            in_specs=[smem] + [pl.BlockSpec(memory_space=pl.ANY)] * 2 + [vmem] * (2 + heads),
            out_specs=[vmem] * heads,
            scratch_shapes=[
                pltpu.VMEM((heads, 1, span), f32),
                pltpu.VMEM((heads, 1, span), f32),
                pltpu.VMEM((heads, hd, span), f32),
                pltpu.VMEM((2, 1, span), f32),
                pltpu.VMEM((blk, span), f32),
                pltpu.VMEM((blk, span), f32),
                pltpu.VMEM((slots, hd), bf16),
                pltpu.VMEM((hd, slots), bf16),
                pltpu.VMEM((heads, 2 * hd, span), bf16),
                pltpu.VMEM((2, blk, hd), bf16),
                pltpu.SemaphoreType.DMA((2,)),
            ],
            out_shape=[jax.ShapeDtypeStruct((tile_rows, span), bf16)] * heads,
            cost_estimate=pl.CostEstimate(
                flops=4 * heads * span * slots * hd,
                transcendentals=heads * span * slots,
                bytes_accessed=4 * slots * hd,
            ),
            name="attend",
        )(lengths, k_rot, v_t, k_new, v_new, *[queries[k] for k in ks])

    far_ks = list(range(far, n))
    near_ks = list(range(far))
    partial = dict(zip(far_ks, attend(1, far_ks)))
    merged_in = {k: xor_send(partial[k], "seq", n, k) for k in far_ks}
    partial.update(zip(near_ks, attend(0, near_ks)))
    for k in near_ks[1:]:
        merged_in[k] = xor_send(partial[k], "seq", n, k)
    merged_in[0] = partial[0]
    attended = pl.pallas_call(
        functools.partial(merge_kernel, n, hd),
        out_shape=jax.ShapeDtypeStruct((hd, span), bf16),
        in_specs=[vmem] * n,
        out_specs=vmem,
        name="merge",
    )(*[merged_in[k] for k in range(n)])

    gathered = {0: attended}
    for k in order:
        gathered[k] = xor_send(attended, "seq", n, k)
    cols = w_out.shape[1]
    outs = pl.pallas_call(
        functools.partial(output_kernel, n, parts, hd),
        out_shape=[jax.ShapeDtypeStruct((span // parts, cols), bf16)] * parts,
        in_specs=[vmem] * (1 + n),
        out_specs=[vmem] * parts,
        scratch_shapes=[pltpu.VMEM((span, cols), f32)],
        name="outproj",
    )(w_out, *[gathered[k] for k in range(n)])
    total = outs[0].astype(f32)
    for j in range(1, parts):
        total = total + xor_send(outs[j], "head", parts, j).astype(f32)
    return total.astype(bf16)


def rope_parts(positions, head_dim):
    angles = positions[:, None] * jnp.asarray(frequencies(head_dim), f32)[None, :]
    return (jnp.cos(angles) * magnitude(), jnp.sin(angles) * magnitude())


def rotate(vectors, cosine, sine_part):
    half_dim = vectors.shape[-1] // 2
    lower_half = vectors[..., :half_dim]
    upper_half = vectors[..., half_dim:]
    cosine = cosine[:, None, :]
    sine_part = sine_part[:, None, :]
    return jnp.concatenate(
        [
            lower_half * cosine - upper_half * sine_part,
            upper_half * cosine + lower_half * sine_part,
        ],
        -1,
    )


def round_trip(values):
    return lax.optimization_barrier(values.astype(bf16)).astype(f32)


def attend_block(running, queries, key_block, value_block, visible):
    maxima, totals, weighted = running
    scores = jnp.einsum("tgrd,kgd->grtk", queries, key_block, preferred_element_type=f32)
    scores = jnp.where(visible, scores, negative)
    new_max = jnp.maximum(maxima, jnp.max(scores, axis=-1))
    probability = jnp.where(visible, jnp.exp(scores - new_max[..., None]), 0.0)
    rescale = jnp.exp(maxima - new_max)
    totals = totals * rescale + jnp.sum(probability, axis=-1)
    weighted = weighted * rescale[..., None] + jnp.einsum(
        "grtk,kgd->grtd", probability.astype(bf16), value_block, preferred_element_type=f32
    )
    return (new_max, totals, weighted)


def general_local(
    hidden_in, norm_gain, w_query, w_key, w_value, w_out, cache_keys, cache_values, lengths, span_start
):
    seq_count = lax.axis_size("seq")
    my_index = lax.axis_index("seq")
    span_len = hidden_in.shape[0]
    width = hidden_in.shape[1] * seq_count
    local_kv = cache_keys.shape[1]
    head_dim = cache_keys.shape[2]
    group_size = w_query.shape[1] // (local_kv * head_dim)
    kv_cols = w_key.shape[1]
    row_count = span_len // seq_count
    first_new = my_index * row_count
    input_f32 = hidden_in.astype(f32)
    square_sums = lax.psum(jnp.sum(input_f32 * input_f32, axis=1), "seq")
    inv_rms = lax.rsqrt(square_sums[:, None] / width + epsilon)
    normed = (input_f32 * inv_rms * norm_gain.astype(f32)).astype(bf16)
    queries = lax.psum(jnp.dot(normed, w_query, preferred_element_type=f32), "seq")
    kv_own = lax.psum_scatter(
        jnp.concatenate(
            [
                jnp.dot(normed, w_key, preferred_element_type=f32),
                jnp.dot(normed, w_value, preferred_element_type=f32),
            ],
            1,
        ),
        "seq",
        scatter_dimension=0,
        tiled=True,
    )
    key_own = kv_own[:, :kv_cols]
    value_own = kv_own[:, kv_cols:]
    shard_ids = jnp.arange(lengths.shape[0], dtype=jnp.int32)
    offset = jnp.sum(jnp.where(shard_ids < my_index, lengths, 0))
    live_count = jnp.sum(jnp.where(shard_ids == my_index, lengths, 0))
    first_pos = jnp.sum(lengths) + span_start[0]
    query_pos = (first_pos + jnp.arange(span_len, dtype=jnp.int32)).astype(f32)
    cosine, sine_part = rope_parts(query_pos, head_dim)
    rotated = rotate(
        queries.reshape(span_len, local_kv * group_size, head_dim), cosine, sine_part
    ) * head_dim ** (-0.5)
    query_low = rotated.astype(bf16).reshape(span_len, local_kv, group_size, head_dim)
    my_keys = round_trip(key_own).reshape(row_count, local_kv, head_dim)
    my_values = value_own.astype(bf16).reshape(row_count, local_kv, head_dim)
    new_pos = (first_pos + first_new + jnp.arange(row_count, dtype=jnp.int32)).astype(f32)
    new_cos, new_sin = rope_parts(new_pos, head_dim)
    new_key_rot = rotate(my_keys, new_cos, new_sin).astype(bf16)
    block_len = math.gcd(cache_keys.shape[0], 1024)

    def sweep_block(block_index, running):
        block_start = block_index * block_len
        key_block = lax.dynamic_slice_in_dim(cache_keys, block_start, block_len, 0).astype(f32)
        value_block = lax.dynamic_slice_in_dim(cache_values, block_start, block_len, 0)
        slot_ids = block_start + jnp.arange(block_len, dtype=jnp.int32)
        occupied = slot_ids < live_count
        positions = (offset + slot_ids).astype(f32)
        block_cos, block_sin = rope_parts(positions, head_dim)
        block_keys = rotate(key_block, block_cos, block_sin).astype(bf16)
        return attend_block(
            running, query_low, block_keys, value_block, occupied[None, None, None, :]
        )

    running = (
        jnp.full((local_kv, group_size, span_len), negative, f32),
        jnp.zeros((local_kv, group_size, span_len), f32),
        jnp.zeros((local_kv, group_size, span_len, head_dim), f32),
    )
    running = lax.fori_loop(0, cache_keys.shape[0] // block_len, sweep_block, running)
    query_rows = jnp.arange(span_len, dtype=jnp.int32)[:, None]
    key_rows = first_new + jnp.arange(row_count, dtype=jnp.int32)[None, :]
    maxima, totals, weighted = attend_block(
        running, query_low, new_key_rot, my_values, (key_rows <= query_rows)[None, None]
    )
    global_max = lax.pmax(maxima, "seq")
    rescale = jnp.exp(maxima - global_max)
    totals, weighted = lax.psum((totals * rescale, weighted * rescale[..., None]), "seq")
    attended = (
        (weighted / totals[..., None])
        .transpose(2, 0, 1, 3)
        .reshape(span_len, local_kv * group_size * head_dim)
    )
    partial_out = jnp.dot(attended.astype(bf16), w_out, preferred_element_type=f32)
    return lax.psum_scatter(partial_out.astype(bf16), "head", scatter_dimension=0, tiled=True)


def local(hidden_in, norm_gain, w_query, w_key, w_value, w_out, cache_keys, cache_values, lengths, span_start):
    args = (
        hidden_in, norm_gain, w_query, w_key, w_value, w_out, cache_keys, cache_values, lengths, span_start
    )
    n, parts = lax.axis_size("seq"), lax.axis_size("head")
    span = hidden_in.shape[0]
    slots, kv_heads, hd = cache_keys.shape
    fits = (
        n & (n - 1) == 0
        and parts & (parts - 1) == 0
        and kv_heads == 2
        and w_query.shape[1] == n * hd
        and kv_heads * hd == span
        and hd % 128 == 0
        and span % (32 * n) == 0
        and span % (16 * parts) == 0
        and slots % 2048 == 0
        and (n // 2) % 2 == 0
    )
    return (fast_local if fits else general_local)(*args)


def solution(mesh):
    return jax.shard_map(
        local,
        mesh=mesh,
        in_specs=(
            P(None, "seq"),
            P(None, "seq"),
            P("seq", "head"),
            P("seq", "head"),
            P("seq", "head"),
            P("head", "seq"),
            P("seq", "head", None),
            P("seq", "head", None),
            P(),
            P(),
        ),
        out_specs=P("head", "seq"),
        check_vma=False,
    )
```

```python
import functools
import math

import jax
import jax.numpy as jnp
import numpy as np
from jax import lax
from jax.experimental import pallas as pl
from jax.experimental.pallas import tpu as pltpu
from jax.sharding import PartitionSpec as P


rope_base = 500000.0
stretch = 64.0
initial_context = 8192.0
ramp_low = 1.0
ramp_high = 32.0
epsilon = 1e-05
negative = -1e30
LOG2E = math.log2(math.e)

f32 = jnp.float32
bf16 = jnp.bfloat16


def frequencies(head_dim):
    half = head_dim // 2
    base = rope_base ** (-2.0 * np.arange(half, dtype=np.float64) / head_dim)
    turns = initial_context * base / (2.0 * np.pi)
    share = np.clip((turns - ramp_low) / (ramp_high - ramp_low), 0.0, 1.0)
    return (1.0 - share) * base / stretch + share * base


def magnitude():
    return 0.1 * math.log(stretch) + 1.0


def split3(v):
    hi = v.astype(bf16).astype(f32)
    mid = (v - hi).astype(bf16).astype(f32)
    return hi, mid, v - hi - mid


def pack_rows(v):
    hi, mid, lo = split3(v)
    rows = lax.broadcasted_iota(jnp.int32, (16, v.shape[1]), 0)
    out = jnp.where(rows == 0, hi, jnp.where(rows == 1, mid, jnp.where(rows == 2, lo, 0.0)))
    return out.astype(bf16)


def unpack_rows(tile):
    t = tile.astype(f32)
    return t[0:1] + t[1:2] + t[2:3]


def turn(a, b):
    return a[0] * b[0] - a[1] * b[1], a[1] * b[0] + a[0] * b[1]


def phase_row(position, bc_ref, bs_ref):
    bits = bc_ref.shape[0]
    place = lax.broadcasted_iota(jnp.int32, bc_ref.shape, 0)
    on = jnp.bitwise_and(jnp.right_shift(jnp.full(bc_ref.shape, position, jnp.int32), place), 1) == 1
    c = jnp.where(on, bc_ref[...], 1.0)
    s = jnp.where(on, bs_ref[...], 0.0)
    while bits > 1:
        bits //= 2
        c, s = turn((c[:bits], s[:bits]), (c[bits:], s[bits:]))
    return c, s


def length_sums(n, me, len_ref):
    offset, total = jnp.int32(0), jnp.int32(0)
    for r in range(n):
        offset = offset + jnp.where(r < me, len_ref[r], 0)
        total = total + len_ref[r]
    return offset, total


def project_kernel(n, hd, x_ref, g_ref, wq_ref, wk_ref, wv_ref, *refs):
    outs, kv = refs[:n], refs[n]
    me = lax.axis_index("seq")
    span = x_ref.shape[0]
    rows = span // n
    x = x_ref[...].astype(f32)
    xg = (x * g_ref[...].astype(f32)).astype(bf16)
    sq = x * x
    hi = sq.astype(bf16)
    lo = (sq - hi.astype(f32)).astype(bf16)
    ones = jnp.ones((16, x.shape[1]), bf16)
    dims = (((1,), (1,)), ((), ()))
    sums = lax.dot_general(ones, hi, dims, preferred_element_type=f32)
    sums = sums + lax.dot_general(ones, lo, dims, preferred_element_type=f32)
    tail = pack_rows(sums[0:1])
    kw = wk_ref.shape[1]
    kv[:, :kw] = jnp.dot(xg, wk_ref[...], preferred_element_type=f32)
    kv[:, kw:] = jnp.dot(xg, wv_ref[...], preferred_element_type=f32)
    for k in range(n):
        peer = jnp.bitwise_xor(me, k)
        col = pl.multiple_of(peer * hd, hd)
        part = jnp.dot(xg, wq_ref[:, pl.ds(col, hd)], preferred_element_type=f32)
        outs[k][:hd, :] = part.T.astype(bf16)
        row = pl.multiple_of(peer * rows, rows)
        outs[k][hd : hd + rows, :] = kv[pl.ds(row, rows), :kw].astype(bf16)
        outs[k][hd + rows : hd + 2 * rows, :] = kv[pl.ds(row, rows), kw:].astype(bf16)
        outs[k][hd + 2 * rows :, :] = tail


def combine_kernel(hd, body, *refs):
    blocks, out = refs[:-1], refs[-1]
    out[:body, :] = functools.reduce(jnp.add, [b[:body, :].astype(f32) for b in blocks]).astype(bf16)
    out[body:, :] = pack_rows(functools.reduce(jnp.add, [unpack_rows(b[body:, :]) for b in blocks]))


def rotate_kernel(
    n, hd, width, len_ref, start_ref, tc_ref, ts_ref, nc_ref, ns_ref, bc_ref, bs_ref, *refs
):
    blocks, (q_ref, k_ref, v_ref) = refs[:-4], refs[-3:]
    me = lax.axis_index("seq")
    half = hd // 2
    span = q_ref.shape[1]
    rows = k_ref.shape[0]
    _, total_len = length_sums(n, me, len_ref)
    pc, ps = phase_row(total_len + start_ref[0], bc_ref, bs_ref)
    pc, ps = pc * magnitude(), ps * magnitude()
    q = blocks[0][:hd, :].astype(f32)
    kv = blocks[0][hd : hd + 2 * rows, :].astype(f32)
    total = unpack_rows(blocks[0][hd + 2 * rows :, :])
    for b in blocks[1:]:
        q = q + b[:hd, :].astype(f32)
        kv = kv + b[hd : hd + 2 * rows, :].astype(f32)
        total = total + unpack_rows(b[hd + 2 * rows :, :])
    inv = lax.rsqrt(total / width + epsilon)
    diag = lax.broadcasted_iota(jnp.int32, (half, hd), 0) == lax.broadcasted_iota(
        jnp.int32, (half, hd), 1
    )
    column = lambda r: jnp.sum(
        jnp.where(diag, jnp.broadcast_to(r, (half, hd)), 0.0), axis=1, keepdims=True
    )
    c, s = turn((column(pc), column(ps)), (tc_ref[...], ts_ref[...]))
    gain = inv * (hd ** (-0.5) * LOG2E)
    lo, up = q[:half] * gain, q[half:] * gain
    q_ref[:half, :] = (lo * c - up * s).astype(bf16)
    q_ref[half:, :] = (up * c + lo * s).astype(bf16)
    lanes = lax.broadcasted_iota(jnp.int32, (rows, span), 1)
    subs = lax.broadcasted_iota(jnp.int32, (rows, span), 0)
    pick = jnp.where(lanes == subs + me * rows, jnp.broadcast_to(inv, (rows, span)), 0.0)
    col = jnp.sum(pick, axis=1, keepdims=True)
    key = (kv[:rows] * col).astype(bf16).astype(f32)
    val = kv[rows:] * col
    mine = pl.ds(pl.multiple_of(me * rows, rows), rows)
    kc, ks = turn((pc, ps), (nc_ref[mine, :], ns_ref[mine, :]))
    ks = jnp.where(lax.broadcasted_iota(jnp.int32, (rows, hd), 1) < half, -ks, ks)
    for g in range(k_ref.shape[1] // hd):
        u = key[:, g * hd : (g + 1) * hd]
        k_ref[:, g * hd : (g + 1) * hd] = (u * kc + pltpu.roll(u, half, 1) * ks).astype(bf16)
    v_ref[...] = val.T.astype(bf16)


def prepare_kernel(
    n, hd, len_ref, ac_ref, as_ref, fc_ref, fs_ref, bc_ref, bs_ref, k_ref, v_ref, after_ref, kr_ref, vt_ref
):
    me = lax.axis_index("seq")
    at = pl.program_id(0)
    blk = kr_ref.shape[1]
    fine = fc_ref.shape[0]
    half = hd // 2
    pair = 2 * hd
    offset, _ = length_sums(n, me, len_ref)

    @pl.when(at * blk < len_ref[me])
    def _():
        pc, ps = phase_row(offset, bc_ref, bs_ref)
        pc, ps = pc * magnitude(), ps * magnitude()
        fc, fs = fc_ref[...], fs_ref[...]
        sign = jnp.where(lax.broadcasted_iota(jnp.int32, (1, hd), 1) < half, -1.0, 1.0)
        r = lax.broadcasted_iota(jnp.int32, (pair, pair), 0)
        c = lax.broadcasted_iota(jnp.int32, (pair, pair), 1)
        perm = jnp.where(c == 2 * (r % hd) + r // hd, 1.0, 0.0).astype(bf16)
        for j in range(blk // hd):
            cos, sin = [], []
            for t in range(hd // fine):
                row = pl.ds(at * (blk // fine) + j * (hd // fine) + t, 1)
                base = turn((pc, ps), (ac_ref[row, :], as_ref[row, :]))
                cc, ss = turn(base, (fc, fs))
                cos.append(cc)
                sin.append(ss * sign)
            cos, sin = jnp.concatenate(cos, 0), jnp.concatenate(sin, 0)
            part = slice(j * hd, (j + 1) * hd)
            u = jnp.dot(perm, k_ref[j * pair : (j + 1) * pair, :], preferred_element_type=f32)
            w = jnp.dot(perm, v_ref[j * pair : (j + 1) * pair, :], preferred_element_type=f32)
            w = w.astype(bf16)
            for g in range(2):
                x = u[g * hd : (g + 1) * hd]
                kr_ref[g, part, :] = (x * cos + pltpu.roll(x, half, 1) * sin).astype(bf16)
                vt_ref[g, :, part] = w[g * hd : (g + 1) * hd].T


def attend_kernel(far, flip, heads, blk, nch, len_ref, kr_hbm, vt_hbm, kn_ref, vn_ref, *refs):
    qs, outs = refs[:heads], refs[-11 - heads : -11]
    m_ref, l_ref, acc_ref, mx_ref, sa, sb, k_ref, v_ref, qx_ref, bias_ref, sem = refs[-11:]
    me = lax.axis_index("seq")
    g = jnp.bitwise_xor(me // far, flip)
    live = len_ref[me]
    hd, span = qs[0].shape
    rows = kn_ref.shape[0]
    ch = blk // nch
    count = pl.cdiv(live, blk)
    copy_k = pltpu.make_async_copy(kr_hbm.at[g], k_ref, sem.at[0])
    copy_v = pltpu.make_async_copy(vt_hbm.at[g], v_ref, sem.at[1])
    copy_k.start()
    copy_v.start()
    m_ref[...] = jnp.full_like(m_ref, negative)
    l_ref[...] = jnp.zeros_like(l_ref)
    acc_ref[...] = jnp.zeros_like(acc_ref)
    unit = jnp.where(lax.broadcasted_iota(jnp.int32, (hd, span), 0) == 0, 1.0, 0.0).astype(bf16)
    for i in range(heads):
        qx_ref[i, :hd, :] = qs[i][...]
        qx_ref[i, hd:, :] = unit
    slot = lax.broadcasted_iota(jnp.int32, (blk, hd), 0) + (count - 1) * blk
    lane = lax.broadcasted_iota(jnp.int32, (blk, hd), 1)
    bias_ref[0] = jnp.zeros((blk, hd), bf16)
    bias_ref[1] = jnp.where((lane == 0) & (slot >= live), negative, 0.0).astype(bf16)
    copy_k.wait()
    copy_v.wait()
    bufs = (sa, sb)

    def score(i, buf, j, c):
        at = pl.multiple_of(j * blk + c * ch, ch)
        last = (j == count - 1).astype(jnp.int32)
        keys = jnp.concatenate([k_ref[pl.ds(at, ch), :], bias_ref[last, c * ch : (c + 1) * ch, :]], 1)
        s = jnp.dot(keys, qx_ref[i], preferred_element_type=f32)
        buf[c * ch : (c + 1) * ch, :] = s
        return jnp.max(s, axis=0, keepdims=True)

    def stage(i, j, i_next, j_next):
        cur, nxt = bufs[i % 2], bufs[(i + 1) % 2]
        old = m_ref[i]
        new = jnp.maximum(old, mx_ref[i % 2])
        scale = jnp.exp2(old - new)
        m_ref[i] = new
        tot, acc, top = l_ref[i] * scale, acc_ref[i] * scale, None
        for c in range(nch):
            t = score(i_next, nxt, j_next, c)
            top = t if top is None else jnp.maximum(top, t)
            p = jnp.exp2(cur[c * ch : (c + 1) * ch, :] - new)
            tot = tot + jnp.sum(p, axis=0, keepdims=True)
            at = pl.multiple_of(j * blk + c * ch, ch)
            acc = acc + jnp.dot(v_ref[:, pl.ds(at, ch)], p.astype(bf16), preferred_element_type=f32)
        l_ref[i], acc_ref[i], mx_ref[(i + 1) % 2] = tot, acc, top

    mx_ref[0] = functools.reduce(jnp.maximum, [score(0, sa, 0, c) for c in range(nch)])

    @pl.loop(0, count)
    def _(j):
        later = jnp.minimum(j + 1, count - 1)
        for i in range(heads):
            stage(i, j, (i + 1) % heads, j if i + 1 < heads else later)

    token = lax.broadcasted_iota(jnp.int32, (rows, span), 1)
    fresh = me * rows + lax.broadcasted_iota(jnp.int32, (rows, span), 0)
    mask = fresh <= token
    cols = pl.ds(pl.multiple_of(g * hd, hd), hd)
    keys, values = kn_ref[:, cols], vn_ref[cols, :]
    for i in range(heads):
        s = jnp.where(mask, jnp.dot(keys, qs[i][...], preferred_element_type=f32), negative)
        old = m_ref[i]
        new = jnp.maximum(old, jnp.max(s, axis=0, keepdims=True))
        p = jnp.where(mask, jnp.exp2(s - new), 0.0)
        scale = jnp.exp2(old - new)
        total = l_ref[i] * scale + jnp.sum(p, axis=0, keepdims=True)
        acc = acc_ref[i] * scale + jnp.dot(values, p.astype(bf16), preferred_element_type=f32)
        outs[i][:hd, :] = (acc / total).astype(bf16)
        outs[i][hd:, :] = pack_rows(new + jnp.log2(total))


def merge_kernel(n, hd, *refs):
    blocks, out = refs[:n], refs[n]
    lse = [unpack_rows(b[hd:, :]) for b in blocks]
    top = functools.reduce(jnp.maximum, lse)
    weights = [jnp.exp2(v - top) for v in lse]
    total = functools.reduce(jnp.add, weights)
    acc = blocks[0][:hd, :].astype(f32) * (weights[0] / total)
    for b, w in zip(blocks[1:], weights[1:]):
        acc = acc + b[:hd, :].astype(f32) * (w / total)
    out[...] = acc.astype(bf16)


def output_kernel(n, parts, hd, w_ref, *refs):
    blocks, outs, acc = refs[:n], refs[n : n + parts], refs[n + parts]
    me, mine = lax.axis_index("seq"), lax.axis_index("head")
    total = None
    for k in range(n):
        row = pl.multiple_of(jnp.bitwise_xor(me, k) * hd, hd)
        a = blocks[k][...].T
        term = jnp.dot(a, w_ref[pl.ds(row, hd), :], preferred_element_type=f32)
        total = term if total is None else total + term
    acc[...] = total
    rows = acc.shape[0] // parts
    for j in range(parts):
        at = pl.multiple_of(jnp.bitwise_xor(mine, j) * rows, rows)
        outs[j][...] = acc[pl.ds(at, rows), :].astype(bf16)


def xor_send(value, axis, size, k):
    return lax.ppermute(value, axis, [(i, i ^ k) for i in range(size)])


def spread(value, n, far, near_order):
    blocks = {0: value, far: xor_send(value, "seq", n, far)}
    for base in (0, far):
        for k in near_order:
            blocks[base ^ k] = xor_send(blocks[base], "seq", n, k)
    return blocks


def limit(mib):
    return pltpu.CompilerParams(vmem_limit_bytes=mib << 20)


def circle(positions, freq):
    angles = np.asarray(positions, np.float64)[:, None] * np.concatenate([freq, freq])[None, :]
    return jnp.asarray(np.cos(angles), f32), jnp.asarray(np.sin(angles), f32)


def fast_local(
    hidden_in, norm_gain, w_query, w_key, w_value, w_out, cache_keys, cache_values, lengths, span_start
):
    n = lax.axis_size("seq")
    parts = lax.axis_size("head")
    span, width_local = hidden_in.shape
    slots, kv_heads, hd = cache_keys.shape
    half = hd // 2
    rows = span // n
    kw = kv_heads * hd
    far = n // 2
    width = width_local * n
    vmem = pl.BlockSpec(memory_space=pltpu.VMEM)
    smem = pl.BlockSpec(memory_space=pltpu.SMEM)

    freq = frequencies(hd)
    fine = 64
    b_cos, b_sin = circle(2.0 ** np.arange(32), freq)
    a_cos, a_sin = circle(fine * np.arange(slots // fine), freq)
    f_cos, f_sin = circle(np.arange(fine), freq)
    n_cos, n_sin = circle(np.arange(span), freq)
    t_cos, t_sin = n_cos[:, :half].T, n_sin[:, :half].T

    block_rows = hd + 2 * rows + 16
    sends = pl.pallas_call(
        functools.partial(project_kernel, n, hd),
        out_shape=[jax.ShapeDtypeStruct((block_rows, span), bf16)] * n,
        in_specs=[vmem] * 5,
        out_specs=[vmem] * n,
        scratch_shapes=[pltpu.VMEM((span, 2 * kw), f32)],
        compiler_params=limit(12),
        name="project",
    )(hidden_in, norm_gain, w_query, w_key, w_value)
    near_order = [k for k in range(2, far)] + [1]
    toward = [sends[far]] + [xor_send(sends[far ^ k], "seq", n, k) for k in near_order]
    got = [sends[0]] + [xor_send(sends[k], "seq", n, k) for k in near_order]
    body = hd + 2 * rows
    across = pl.pallas_call(
        functools.partial(combine_kernel, hd, body),
        out_shape=jax.ShapeDtypeStruct((block_rows, span), bf16),
        in_specs=[vmem] * far,
        out_specs=vmem,
        compiler_params=limit(6),
        name="combine",
    )(*toward)
    got.append(xor_send(across, "seq", n, far))

    step = 2048
    whole = lambda i: (0, 0)
    consts = (a_cos, a_sin, f_cos, f_sin, b_cos, b_sin)
    k_rot, v_t = pl.pallas_call(
        functools.partial(prepare_kernel, n, hd),
        grid=(slots // step,),
        in_specs=[smem]
        + [pl.BlockSpec(v.shape, whole) for v in consts]
        + [pl.BlockSpec((step * kv_heads, hd), lambda i: (i, 0))] * 2
        + [pl.BlockSpec(memory_space=pl.ANY)],
        out_specs=[
            pl.BlockSpec((kv_heads, step, hd), lambda i: (0, i, 0)),
            pl.BlockSpec((kv_heads, hd, step), lambda i: (0, 0, i)),
        ],
        out_shape=[
            jax.ShapeDtypeStruct((kv_heads, slots, hd), bf16),
            jax.ShapeDtypeStruct((kv_heads, hd, slots), bf16),
        ],
        cost_estimate=pl.CostEstimate(
            flops=8 * slots * kw, transcendentals=0, bytes_accessed=8 * slots * kw
        ),
        compiler_params=limit(16),
        name="prepare",
    )(
        lengths,
        *consts,
        cache_keys.reshape(slots * kv_heads, hd),
        cache_values.reshape(slots * kv_heads, hd),
        across,
    )

    q_own, k_new, v_new = pl.pallas_call(
        functools.partial(rotate_kernel, n, hd, width),
        out_shape=[
            jax.ShapeDtypeStruct((hd, span), bf16),
            jax.ShapeDtypeStruct((rows, kw), bf16),
            jax.ShapeDtypeStruct((kw, rows), bf16),
        ],
        in_specs=[smem] * 2 + [vmem] * (6 + len(got)) + [pl.BlockSpec(memory_space=pl.ANY)],
        out_specs=[vmem] * 3,
        compiler_params=limit(8),
        name="rotate",
    )(lengths, span_start, t_cos, t_sin, n_cos, n_sin, b_cos, b_sin, *got, k_rot)

    queries = spread(q_own, n, far, near_order)

    tile_rows = hd + 16
    blk, nch = 1024, 4

    def attend(flip, ks, after):
        heads = len(ks)
        return pl.pallas_call(
            functools.partial(attend_kernel, far, flip, heads, blk, nch),
            in_specs=[smem] + [pl.BlockSpec(memory_space=pl.ANY)] * 2 + [vmem] * (2 + heads)
            + [pl.BlockSpec(memory_space=pl.ANY)] * len(after),
            out_specs=[vmem] * heads,
            scratch_shapes=[
                pltpu.VMEM((heads, 1, span), f32),
                pltpu.VMEM((heads, 1, span), f32),
                pltpu.VMEM((heads, hd, span), f32),
                pltpu.VMEM((2, 1, span), f32),
                pltpu.VMEM((blk, span), f32),
                pltpu.VMEM((blk, span), f32),
                pltpu.VMEM((slots, hd), bf16),
                pltpu.VMEM((hd, slots), bf16),
                pltpu.VMEM((heads, 2 * hd, span), bf16),
                pltpu.VMEM((2, blk, hd), bf16),
                pltpu.SemaphoreType.DMA((2,)),
            ],
            out_shape=[jax.ShapeDtypeStruct((tile_rows, span), bf16)] * heads,
            cost_estimate=pl.CostEstimate(
                flops=4 * heads * span * slots * hd,
                transcendentals=heads * span * slots,
                bytes_accessed=4 * slots * hd,
            ),
            compiler_params=limit(16),
            name="attend",
        )(lengths, k_rot, v_t, k_new, v_new, *[queries[k] for k in ks], *after)

    far_ks = list(range(far, n))
    near_ks = list(range(far))
    partial = dict(zip(far_ks, attend(1, far_ks, ())))
    merged_in = {k: xor_send(partial[k], "seq", n, k) for k in far_ks}
    partial.update(zip(near_ks, attend(0, near_ks, (partial[far],))))
    for k in near_ks[1:]:
        merged_in[k] = xor_send(partial[k], "seq", n, k)
    merged_in[0] = partial[0]
    attended = pl.pallas_call(
        functools.partial(merge_kernel, n, hd),
        out_shape=jax.ShapeDtypeStruct((hd, span), bf16),
        in_specs=[vmem] * n,
        out_specs=vmem,
        compiler_params=limit(6),
        name="merge",
    )(*[merged_in[k] for k in range(n)])

    gathered = spread(attended, n, far, near_order)
    cols = w_out.shape[1]
    outs = pl.pallas_call(
        functools.partial(output_kernel, n, parts, hd),
        out_shape=[jax.ShapeDtypeStruct((span // parts, cols), bf16)] * parts,
        in_specs=[vmem] * (1 + n),
        out_specs=[vmem] * parts,
        scratch_shapes=[pltpu.VMEM((span, cols), f32)],
        compiler_params=limit(8),
        name="outproj",
    )(w_out, *[gathered[k] for k in range(n)])
    total = outs[0].astype(f32)
    for j in range(1, parts):
        total = total + xor_send(outs[j], "head", parts, j).astype(f32)
    return total.astype(bf16)


def rope_parts(positions, head_dim):
    angles = positions[:, None] * jnp.asarray(frequencies(head_dim), f32)[None, :]
    return (jnp.cos(angles) * magnitude(), jnp.sin(angles) * magnitude())


def rotate(vectors, cosine, sine_part):
    half_dim = vectors.shape[-1] // 2
    lower_half = vectors[..., :half_dim]
    upper_half = vectors[..., half_dim:]
    cosine = cosine[:, None, :]
    sine_part = sine_part[:, None, :]
    return jnp.concatenate(
        [
            lower_half * cosine - upper_half * sine_part,
            upper_half * cosine + lower_half * sine_part,
        ],
        -1,
    )


def round_trip(values):
    return lax.optimization_barrier(values.astype(bf16)).astype(f32)


def attend_block(running, queries, key_block, value_block, visible):
    maxima, totals, weighted = running
    scores = jnp.einsum("tgrd,kgd->grtk", queries, key_block, preferred_element_type=f32)
    scores = jnp.where(visible, scores, negative)
    new_max = jnp.maximum(maxima, jnp.max(scores, axis=-1))
    probability = jnp.where(visible, jnp.exp(scores - new_max[..., None]), 0.0)
    rescale = jnp.exp(maxima - new_max)
    totals = totals * rescale + jnp.sum(probability, axis=-1)
    weighted = weighted * rescale[..., None] + jnp.einsum(
        "grtk,kgd->grtd", probability.astype(bf16), value_block, preferred_element_type=f32
    )
    return (new_max, totals, weighted)


def general_local(
    hidden_in, norm_gain, w_query, w_key, w_value, w_out, cache_keys, cache_values, lengths, span_start
):
    seq_count = lax.axis_size("seq")
    my_index = lax.axis_index("seq")
    span_len = hidden_in.shape[0]
    width = hidden_in.shape[1] * seq_count
    local_kv = cache_keys.shape[1]
    head_dim = cache_keys.shape[2]
    group_size = w_query.shape[1] // (local_kv * head_dim)
    kv_cols = w_key.shape[1]
    row_count = span_len // seq_count
    first_new = my_index * row_count
    input_f32 = hidden_in.astype(f32)
    square_sums = lax.psum(jnp.sum(input_f32 * input_f32, axis=1), "seq")
    inv_rms = lax.rsqrt(square_sums[:, None] / width + epsilon)
    normed = (input_f32 * inv_rms * norm_gain.astype(f32)).astype(bf16)
    queries = lax.psum(jnp.dot(normed, w_query, preferred_element_type=f32), "seq")
    kv_own = lax.psum_scatter(
        jnp.concatenate(
            [
                jnp.dot(normed, w_key, preferred_element_type=f32),
                jnp.dot(normed, w_value, preferred_element_type=f32),
            ],
            1,
        ),
        "seq",
        scatter_dimension=0,
        tiled=True,
    )
    key_own = kv_own[:, :kv_cols]
    value_own = kv_own[:, kv_cols:]
    shard_ids = jnp.arange(lengths.shape[0], dtype=jnp.int32)
    offset = jnp.sum(jnp.where(shard_ids < my_index, lengths, 0))
    live_count = jnp.sum(jnp.where(shard_ids == my_index, lengths, 0))
    first_pos = jnp.sum(lengths) + span_start[0]
    query_pos = (first_pos + jnp.arange(span_len, dtype=jnp.int32)).astype(f32)
    cosine, sine_part = rope_parts(query_pos, head_dim)
    rotated = rotate(
        queries.reshape(span_len, local_kv * group_size, head_dim), cosine, sine_part
    ) * head_dim ** (-0.5)
    query_low = rotated.astype(bf16).reshape(span_len, local_kv, group_size, head_dim)
    my_keys = round_trip(key_own).reshape(row_count, local_kv, head_dim)
    my_values = value_own.astype(bf16).reshape(row_count, local_kv, head_dim)
    new_pos = (first_pos + first_new + jnp.arange(row_count, dtype=jnp.int32)).astype(f32)
    new_cos, new_sin = rope_parts(new_pos, head_dim)
    new_key_rot = rotate(my_keys, new_cos, new_sin).astype(bf16)
    block_len = math.gcd(cache_keys.shape[0], 1024)

    def sweep_block(block_index, running):
        block_start = block_index * block_len
        key_block = lax.dynamic_slice_in_dim(cache_keys, block_start, block_len, 0).astype(f32)
        value_block = lax.dynamic_slice_in_dim(cache_values, block_start, block_len, 0)
        slot_ids = block_start + jnp.arange(block_len, dtype=jnp.int32)
        occupied = slot_ids < live_count
        positions = (offset + slot_ids).astype(f32)
        block_cos, block_sin = rope_parts(positions, head_dim)
        block_keys = rotate(key_block, block_cos, block_sin).astype(bf16)
        return attend_block(
            running, query_low, block_keys, value_block, occupied[None, None, None, :]
        )

    running = (
        jnp.full((local_kv, group_size, span_len), negative, f32),
        jnp.zeros((local_kv, group_size, span_len), f32),
        jnp.zeros((local_kv, group_size, span_len, head_dim), f32),
    )
    running = lax.fori_loop(0, cache_keys.shape[0] // block_len, sweep_block, running)
    query_rows = jnp.arange(span_len, dtype=jnp.int32)[:, None]
    key_rows = first_new + jnp.arange(row_count, dtype=jnp.int32)[None, :]
    maxima, totals, weighted = attend_block(
        running, query_low, new_key_rot, my_values, (key_rows <= query_rows)[None, None]
    )
    global_max = lax.pmax(maxima, "seq")
    rescale = jnp.exp(maxima - global_max)
    totals, weighted = lax.psum((totals * rescale, weighted * rescale[..., None]), "seq")
    attended = (
        (weighted / totals[..., None])
        .transpose(2, 0, 1, 3)
        .reshape(span_len, local_kv * group_size * head_dim)
    )
    partial_out = jnp.dot(attended.astype(bf16), w_out, preferred_element_type=f32)
    return lax.psum_scatter(partial_out.astype(bf16), "head", scatter_dimension=0, tiled=True)


def local(hidden_in, norm_gain, w_query, w_key, w_value, w_out, cache_keys, cache_values, lengths, span_start):
    args = (
        hidden_in, norm_gain, w_query, w_key, w_value, w_out, cache_keys, cache_values, lengths, span_start
    )
    n, parts = lax.axis_size("seq"), lax.axis_size("head")
    span = hidden_in.shape[0]
    slots, kv_heads, hd = cache_keys.shape
    fits = (
        n & (n - 1) == 0
        and parts & (parts - 1) == 0
        and kv_heads == 2
        and w_query.shape[1] == n * hd
        and kv_heads * hd == span
        and hd % 128 == 0
        and span % (32 * n) == 0
        and span % (16 * parts) == 0
        and slots % 2048 == 0
        and (n // 2) % 2 == 0
    )
    return (fast_local if fits else general_local)(*args)


def solution(mesh):
    return jax.shard_map(
        local,
        mesh=mesh,
        in_specs=(
            P(None, "seq"),
            P(None, "seq"),
            P("seq", "head"),
            P("seq", "head"),
            P("seq", "head"),
            P("head", "seq"),
            P("seq", "head", None),
            P("seq", "head", None),
            P(),
            P(),
        ),
        out_specs=P("head", "seq"),
        check_vma=False,
    )
```
